32 devices in a mesh: cfg: 2 (over x), tm: 16 (over z, y, core).
Axes of the slice: x: 2, y: 2, z: 4, core: 2. Of those that a mesh axis runs over, the one named last changes fastest.
Arguments:
- perambulators: bfloat16 [64, 2, 512, 512], P(('cfg', 'tm')), parts along dimension 0, may hold values from -0.1875 to 0.1875
- elementals: bfloat16 [96, 2, 128, 128], P(('cfg', 'tm')), parts along dimension 0, may hold values from -0.375 to 0.375
- elem_place: int32 [96], P('cfg'), parts along dimension 0, may hold values from 0 to 47, as said below
- op_lists: int32 [64, 11], P(('cfg', 'tm')), parts along dimension 0, may hold values from 0 to 47, as said below
Outputs:
- correlators: float32 [64, 2, 6, 5], P(('cfg', 'tm')), parts along dimension 0
The draws below stay inside these ranges and needn't reach their ends.
There are 2 independent parts, one for each index of `cfg`. The reference program is written for one: setup_inputs(seed, part) draws one part's arguments, and reference() takes and returns one part's arrays. A program takes and returns all parts, laid end to end along the dimension named above; each array names one. Nothing has to cross between parts.
Inputs may be any that keep to these rules, and one draw needn't show every extreme that they name: A permutation: every storage row appears once; elemental e is row elem_place[e] of elementals. `op_lists`: over the 2 rows of one device, at most 6 entries name elementals whose storage rows lie on any single device (storage row // 3); in every draw the stored elementals of some device are named exactly 6 times by the rows of every device.
All inputs are finite; a program needn't handle non-finite values.
Results may differ from the reference program's by a relative error of at most 0.0041.
Values may be sent and summed in bfloat16 or wider, within the bound.
No kernel may reach another device: no remote copies, remote signals or barrier semaphores. Data moves between devices by JAX's collectives and lax.ppermute only.
A program may use at most 128 MiB of HBM per device.

```python
import jax
import jax.numpy as jnp
from jax import lax

NEV = 128
NS = 4
ORD = 512
OPS_SRC = 6
OPS_ALL = 11
PAIR_DEV = 2
PAIRS = 32
ELEM_DEV = 3
ELEMS = 48


def request_plan(key):
    owner_total = PAIRS // PAIR_DEV
    row_count = PAIR_DEV * OPS_ALL
    slot_cap = max(2, 5 * row_count // owner_total)
    place_ids = jax.random.permutation(jax.random.fold_in(key, 11), ELEMS).astype(jnp.int32)
    hot_owner = jax.random.randint(jax.random.fold_in(key, 12), (), 0, owner_total, dtype=jnp.int32)
    favour = jax.random.randint(jax.random.fold_in(key, 13), (owner_total,), 0, 4, dtype=jnp.int32)
    owner_grid = jnp.arange(owner_total, dtype=jnp.int32)[:, None] * jnp.ones((1, slot_cap), jnp.int32)
    unique_tail = jnp.arange(owner_total * slot_cap, dtype=jnp.int32).reshape(owner_total, slot_cap)

    def one_device(dev_key):
        noise_int = jax.random.randint(jax.random.fold_in(dev_key, 1), (owner_total, slot_cap), 0, 4096, dtype=jnp.int32)
        score_int = noise_int - favour[:, None] * 512 + jnp.where(owner_grid == hot_owner, 100000, 0)
        score_int = score_int * (owner_total * slot_cap) + unique_tail
        order_idx = jnp.argsort(score_int.reshape(-1))
        chosen = (order_idx[:row_count - slot_cap] // slot_cap).astype(jnp.int32)
        owners = jnp.concatenate([jnp.full((slot_cap,), hot_owner, jnp.int32), chosen])
        owners = owners[jax.random.permutation(jax.random.fold_in(dev_key, 2), row_count)]
        slot_ids = jax.random.randint(jax.random.fold_in(dev_key, 3), (row_count,), 0, ELEM_DEV, dtype=jnp.int32)
        return owners * ELEM_DEV + slot_ids
    device_keys = jax.random.split(jax.random.fold_in(key, 14), owner_total)
    locations = jax.vmap(one_device)(device_keys)
    inverse = jnp.argsort(place_ids).astype(jnp.int32)
    list_ids = inverse[locations].reshape(PAIRS, OPS_ALL).astype(jnp.int32)
    return (place_ids, list_ids)


def draw_elem_place(key, part):
    return request_plan(key)[0]


def draw_op_lists(key, part):
    return request_plan(key)[1]


def block_levels(stream_key, shape, cuts, low, largest):
    gain, own = 1.0, jax.random.fold_in(stream_key, 6)
    for dim, parts in cuts:
        steps = jnp.exp(jax.random.uniform(jax.random.fold_in(own, dim), (parts,), jnp.float32, low / len(cuts), largest / len(cuts)))
        gain = gain * jnp.repeat(steps, shape[dim] // parts).reshape([-1 if axis == dim else 1 for axis in range(len(shape))])
    return gain


def bell_draw(stream_key, extent, spread, most, shards=(), kind=jnp.bfloat16):
    gain = block_levels(stream_key, extent, shards, -0.22, 0.18) if shards else 1.0
    drawn = jax.random.normal(stream_key, extent, jnp.float32) * spread * gain
    return jnp.minimum(jnp.maximum(drawn, -most), most).astype(kind)


def setup_inputs(seed: int = 0, part: int = 0) -> dict:
    streams_of = jax.random.split(jax.random.key(seed), 5)
    own_keys = jax.random.split(jax.random.fold_in(streams_of[4], part), 5)
    return {
        "perambulators": bell_draw(own_keys[0], (PAIRS, 2, ORD, ORD), (1 / (2 * ORD) ** 0.5), 0.1875, ((0, 16),)),
        "elementals": bell_draw(own_keys[1], (ELEMS, 2, NEV, NEV), (1 / (2 * NEV) ** 0.5), 0.375, ((0, 16),)),
        "elem_place": draw_elem_place(jax.random.fold_in(jax.random.fold_in(streams_of[4], part), 71), part),
        "op_lists": draw_op_lists(jax.random.fold_in(jax.random.fold_in(streams_of[4], part), 71), part),
    }


def rounded(values):
    return lax.optimization_barrier(values.astype(jnp.bfloat16)).astype(jnp.float32)


def apply_elementals(phi_real, phi_imag, tau_full):
    tau_blocks = tau_full.reshape(2, NS, NEV, ORD)
    prod_real = jnp.einsum("aij,sjc->asic", phi_real, tau_blocks[0]) - jnp.einsum("aij,sjc->asic", phi_imag, tau_blocks[1])
    prod_imag = jnp.einsum("aij,sjc->asic", phi_real, tau_blocks[1]) + jnp.einsum("aij,sjc->asic", phi_imag, tau_blocks[0])
    count_ops = phi_real.shape[0]
    return rounded(prod_real).reshape(count_ops, ORD, ORD), rounded(prod_imag).reshape(count_ops, ORD, ORD)


def trace_pair(first, second):
    return jnp.einsum("arc,bcr->ab", first, second)


def reference(perambulators, elementals, elem_place, op_lists):
    half_pairs = PAIRS // 2

    def one_pair(pair_idx):
        own_tau = lax.dynamic_index_in_dim(perambulators, pair_idx, 0, keepdims=False).astype(jnp.float32)
        mirror_idx = ((pair_idx + half_pairs) % PAIRS).astype(jnp.int32)
        mirror_tau = lax.dynamic_index_in_dim(perambulators, mirror_idx, 0, keepdims=False).astype(jnp.float32)
        wanted = lax.dynamic_index_in_dim(op_lists, pair_idx, 0, keepdims=False)
        stored_at = elem_place[wanted]
        phi_rows = elementals[stored_at].astype(jnp.float32)
        left_real, left_imag = apply_elementals(phi_rows[:OPS_SRC, 0], phi_rows[:OPS_SRC, 1], own_tau)
        right_real, right_imag = apply_elementals(phi_rows[OPS_SRC:, 0], phi_rows[OPS_SRC:, 1], mirror_tau)
        corr_real = trace_pair(left_real, right_real) - trace_pair(left_imag, right_imag)
        corr_imag = trace_pair(left_real, right_imag) + trace_pair(left_imag, right_real)
        return jnp.stack([corr_real, corr_imag], axis=0)

    return lax.map(one_pair, jnp.arange(PAIRS, dtype=jnp.int32))
```

```python
import functools

import jax
import jax.numpy as jnp
from jax import lax
from jax.experimental import pallas as pl
from jax.experimental.pallas import tpu as pltpu
from jax.sharding import PartitionSpec as P

OPS_SRC = 6
NT = (((1,), (1,)), ((), ()))


def apply_kernel(src, ops, place, half, near, far, tau_t, w_ref, phi_ref, buf, sem, *, per_owner, owners):
    count = ops.shape[0]
    spins, order, twice = tau_t.shape
    ev = twice // 2

    def copies(entry):
        row = place[ops[entry]]
        owner = lax.div(row, per_owner)
        slot = row - owner * per_owner
        side = lax.div(owner, owners)
        at = (owner - side * owners) * per_owner + slot
        here = side == half[0]
        dst = src[entry]
        return (
            here,
            pltpu.make_async_copy(near.at[at], buf.at[dst], sem.at[dst]),
            pltpu.make_async_copy(far.at[at], buf.at[dst], sem.at[dst]),
        )

    def fetch(entry, _):
        here, from_near, from_far = copies(entry)

        @pl.when(here)
        def _():
            from_near.start()

        @pl.when(jnp.logical_not(here))
        def _():
            from_far.start()

        return 0

    def arrive(entry, _):
        pltpu.make_async_copy(near.at[0], buf.at[src[entry]], sem.at[src[entry]]).wait()
        return 0

    lax.fori_loop(0, count, fetch, 0)
    lax.fori_loop(0, count, arrive, 0)

    def product(m, _):
        real = buf[m, 0]
        imag = buf[m, 1]
        lifted = jnp.concatenate(
            [jnp.concatenate([real, -imag], axis=1), jnp.concatenate([imag, real], axis=1)], axis=0
        )
        row = pl.multiple_of(m * ev, ev)
        for inner in range(spins):
            out = lax.dot_general(tau_t[inner], lifted, NT, preferred_element_type=jnp.float32)
            out = out.astype(jnp.bfloat16)
            for outer in range(spins):
                w_ref[outer, pl.ds(row, ev), inner * twice : (inner + 1) * twice] = out[
                    outer * ev : (outer + 1) * ev
                ]
        return 0

    lax.fori_loop(0, count // 2, product, 0)
    phi_ref[...] = buf[count // 2 :].astype(jnp.float32)


def lift_rows(mu, spins):
    ev = mu.shape[1]
    top, low = [], []
    for inner in range(spins):
        real = mu[0, :, inner * ev : (inner + 1) * ev]
        imag = mu[1, :, inner * ev : (inner + 1) * ev]
        top += [real, -imag]
        low += [imag, real]
    return jnp.concatenate([jnp.concatenate(top, axis=1), jnp.concatenate(low, axis=1)], axis=0)


def add_spin(w, mu, z_ref, first, entries):
    ev = mu.shape[1]
    lifted = lift_rows(mu, w.shape[1] // (2 * ev))
    for m in range(entries):
        rows = slice(m * ev, (m + 1) * ev)
        part = lax.dot_general(w[rows], lifted, NT, preferred_element_type=jnp.float32)
        if first is None:
            z_ref[rows] = z_ref[rows] + part
        else:
            z_ref[rows] = jnp.where(first, part, z_ref[rows] + part)


def early_kernel(w_ref, mu_ref, z_ref, *, entries):
    add_spin(w_ref.at[0], mu_ref[:, 0], z_ref, pl.program_id(0) == 0, entries)


def late_kernel(w_ref, mu_ref, z_in, phi_ref, out_ref, z_ref, acc, *, entries):
    ev = mu_ref.shape[2]
    z_ref[...] = z_in[...]
    add_spin(w_ref.at[0], mu_ref[:, 0], z_ref, None, entries)
    sink = entries - OPS_SRC
    spot = 0
    for pair in range(2):
        for a in range(OPS_SRC):
            for b in range(sink):
                m, f = (a, b) if pair == 0 else (OPS_SRC + b, sink + a)
                zr = z_ref[m * ev : (m + 1) * ev, :ev]
                zi = z_ref[m * ev : (m + 1) * ev, ev:]
                fr, fi = phi_ref[f, 0], phi_ref[f, 1]
                for part in range(2):
                    whole = zr * fr - zi * fi if part == 0 else zr * fi + zi * fr
                    at = (pair * 2 + part) * OPS_SRC * sink + a * sink + b
                    acc[at] = jnp.sum(whole.reshape(ev // 8, 8, ev), axis=0)
                    spot += 1
    sums = jnp.sum(jnp.sum(acc[...], axis=1), axis=1, keepdims=True)
    rows = lax.broadcasted_iota(jnp.int32, (spot, 128), 0)
    lanes = lax.broadcasted_iota(jnp.int32, (spot, 128), 1)
    out_ref[...] = jnp.sum(jnp.where(rows == lanes, sums, 0.0), axis=0, keepdims=True)


def shards(perambulators, elementals, elem_place, op_lists):
    size = lax.axis_size("tm")
    half = size // 2
    me = lax.axis_index("tm")
    upper = (me >= half).astype(jnp.int32)
    across = [(source, (source + half) % size) for source in range(size)]
    groups = [list(range(half)), list(range(half, size))]
    list_len = op_lists.shape[1]
    sink = list_len - OPS_SRC
    per_owner, _, ev, _ = elementals.shape
    order = perambulators.shape[2]
    spins = order // ev

    far_own = lax.ppermute(elementals, "tm", across)
    near = lax.all_gather(elementals, "tm", axis_index_groups=groups, tiled=True)
    sent = lax.dynamic_index_in_dim(perambulators, 1 - upper, 0, keepdims=False)
    sent = sent.reshape(2, spins, ev, order)
    mu_a = lax.ppermute(sent[:, : spins - 1], "tm", across)
    mu_b = lax.ppermute(sent[:, spins - 1 :], "tm", across)
    other_list = lax.ppermute(op_lists, "tm", across)
    far = lax.all_gather(far_own, "tm", axis_index_groups=groups, tiled=True)

    kept = lax.dynamic_index_in_dim(perambulators, upper, 0, keepdims=False)
    tau_t = kept.reshape(2, spins, ev, order).transpose(1, 3, 0, 2).reshape(spins, order, 2 * ev)
    ops = jnp.concatenate(
        [
            lax.dynamic_index_in_dim(op_lists, upper, 0, keepdims=False),
            lax.dynamic_index_in_dim(other_list, upper, 0, keepdims=False),
        ]
    )
    target = (
        list(range(OPS_SRC))
        + [list_len + b for b in range(sink)]
        + [list_len + sink + a for a in range(OPS_SRC)]
        + [OPS_SRC + b for b in range(sink)]
    )
    smem = pl.BlockSpec(memory_space=pltpu.SMEM)
    vmem = pl.BlockSpec(memory_space=pltpu.VMEM)
    anyspace = pl.BlockSpec(memory_space=pl.ANY)
    width = list_len * ev
    depth = 2 * order
    w, phi = pl.pallas_call(
        functools.partial(apply_kernel, per_owner=per_owner, owners=half),
        out_shape=(
            jax.ShapeDtypeStruct((spins, width, depth), jnp.bfloat16),
            jax.ShapeDtypeStruct((list_len, 2, ev, ev), jnp.float32),
        ),
        in_specs=[smem, smem, smem, smem, anyspace, anyspace, vmem],
        out_specs=(vmem, vmem),
        scratch_shapes=[
            pltpu.VMEM((2 * list_len, 2, ev, ev), jnp.bfloat16),
            pltpu.SemaphoreType.DMA((2 * list_len,)),
        ],
        compiler_params=pltpu.CompilerParams(vmem_limit_bytes=24 << 20),
        cost_estimate=pl.CostEstimate(
            flops=2 * spins * width * depth * 2 * ev, bytes_accessed=2 * spins * width * depth, transcendentals=0
        ),
        name="apply",
    )(jnp.array(target, jnp.int32), ops, elem_place, upper[None], near, far, tau_t)
    z = pl.pallas_call(
        functools.partial(early_kernel, entries=list_len),
        out_shape=jax.ShapeDtypeStruct((width, 2 * ev), jnp.float32),
        grid=(spins - 1,),
        in_specs=[
            pl.BlockSpec((1, width, depth), lambda s: (s, 0, 0)),
            pl.BlockSpec((2, 1, ev, order), lambda s: (0, s, 0, 0)),
        ],
        out_specs=pl.BlockSpec((width, 2 * ev), lambda s: (0, 0)),
        compiler_params=pltpu.CompilerParams(vmem_limit_bytes=24 << 20),
        cost_estimate=pl.CostEstimate(
            flops=2 * (spins - 1) * width * depth * 2 * ev,
            bytes_accessed=2 * (spins - 1) * width * depth,
            transcendentals=0,
        ),
        name="early",
    )(w, mu_a)
    result = pl.pallas_call(
        functools.partial(late_kernel, entries=list_len),
        out_shape=jax.ShapeDtypeStruct((1, 128), jnp.float32),
        grid=(1,),
        in_specs=[
            pl.BlockSpec((1, width, depth), lambda s: (spins - 1, 0, 0)),
            pl.BlockSpec((2, 1, ev, order), lambda s: (0, 0, 0, 0)),
            pl.BlockSpec((width, 2 * ev), lambda s: (0, 0)),
            pl.BlockSpec((list_len, 2, ev, ev), lambda s: (0, 0, 0, 0)),
        ],
        out_specs=pl.BlockSpec((1, 128), lambda s: (0, 0)),
        scratch_shapes=[
            pltpu.VMEM((width, 2 * ev), jnp.float32),
            pltpu.VMEM((4 * OPS_SRC * sink, 8, ev), jnp.float32),
        ],
        compiler_params=pltpu.CompilerParams(vmem_limit_bytes=24 << 20),
        cost_estimate=pl.CostEstimate(
            flops=2 * width * depth * 2 * ev, bytes_accessed=2 * width * depth, transcendentals=0
        ),
        name="late",
    )(w, mu_b, z, phi)
    pair_len = 2 * OPS_SRC * sink
    own = result[0, :pair_len]
    back = lax.ppermute(result[:, pair_len : 2 * pair_len], "tm", across)[0]
    both = jnp.where(upper == 0, jnp.stack([own, back]), jnp.stack([back, own]))
    return both.reshape(2, 2, OPS_SRC, sink)


def solution(mesh):
    return jax.shard_map(
        shards,
        mesh=mesh,
        in_specs=(
            P(("cfg", "tm"), None, None, None),
            P(("cfg", "tm"), None, None, None),
            P("cfg"),
            P(("cfg", "tm"), None),
        ),
        out_specs=P(("cfg", "tm"), None, None, None),
        check_vma=False,
    )
```

```python
import functools

import jax
import jax.numpy as jnp
from jax import lax
from jax.experimental import pallas as pl
from jax.experimental.pallas import tpu as pltpu
from jax.sharding import PartitionSpec as P

OPS_SRC = 6
NT = (((1,), (1,)), ((), ()))


def apply_kernel(src, ops, place, self_id, tau_t, *refs, per_owner, half):
    *pieces, w_ref, phi_ref, table, sem = refs
    count = ops.shape[0]
    spins, order, twice = tau_t.shape
    ev = twice // 2
    steps = half.bit_length() - 1
    each = pieces[0].shape[0]
    copies = [
        pltpu.make_async_copy(piece, table.at[pl.ds(at * each, each)], sem.at[at]) for at, piece in enumerate(pieces)
    ]
    for copy in copies:
        copy.start()
    for copy in copies:
        copy.wait()

    def entry_of(slot):
        row = place[ops[src[slot]]]
        owner = lax.div(row, per_owner)
        apart = lax.bitwise_xor(owner, self_id[0])
        index = half * (apart >= half).astype(jnp.int32)
        for step in range(steps):
            bit = lax.bitwise_and(lax.shift_right_logical(apart, jnp.int32(steps - 1 - step)), 1)
            index = index + bit * (1 << step)
        return table[index, pl.ds(pl.multiple_of((row - owner * per_owner) * twice, twice), twice)]

    def product(m, _):
        phi = entry_of(m)
        real, imag = phi[:ev], phi[ev:]
        lifted = jnp.concatenate(
            [jnp.concatenate([real, -imag], axis=1), jnp.concatenate([imag, real], axis=1)], axis=0
        )
        row = pl.multiple_of(m * ev, ev)
        for inner in range(spins):
            out = lax.dot_general(tau_t[inner], lifted, NT, preferred_element_type=jnp.float32)
            out = out.astype(jnp.bfloat16)
            for outer in range(spins):
                w_ref[outer, pl.ds(row, ev), inner * twice : (inner + 1) * twice] = out[
                    outer * ev : (outer + 1) * ev
                ]
        return 0

    lax.fori_loop(0, count // 2, product, 0)

    def keep(m, _):
        phi_ref[m] = entry_of(count // 2 + m).astype(jnp.float32)
        return 0

    lax.fori_loop(0, count // 2, keep, 0)


def lift_rows(mu, spins):
    ev = mu.shape[1]
    top, low = [], []
    for inner in range(spins):
        real = mu[0, :, inner * ev : (inner + 1) * ev]
        imag = mu[1, :, inner * ev : (inner + 1) * ev]
        top += [real, -imag]
        low += [imag, real]
    return jnp.concatenate([jnp.concatenate(top, axis=1), jnp.concatenate(low, axis=1)], axis=0)


def add_spin(w, mu, z_ref, first, entries):
    ev = mu.shape[1]
    lifted = lift_rows(mu, w.shape[1] // (2 * ev))
    for m in range(entries):
        rows = slice(m * ev, (m + 1) * ev)
        part = lax.dot_general(w[rows], lifted, NT, preferred_element_type=jnp.float32)
        if first is None:
            z_ref[rows] = z_ref[rows] + part
        else:
            z_ref[rows] = jnp.where(first, part, z_ref[rows] + part)


def early_kernel(w_ref, mu_ref, z_ref, *, entries):
    add_spin(w_ref.at[0], mu_ref[:, 0], z_ref, pl.program_id(0) == 0, entries)


def late_kernel(w_ref, mu_ref, z_in, phi_ref, own_ref, other_ref, z_ref, acc, *, entries):
    ev = mu_ref.shape[2]
    z_ref[...] = z_in[...]
    add_spin(w_ref.at[0], mu_ref[:, 0], z_ref, None, entries)
    sink = entries - OPS_SRC
    rows = 4 * sink
    for pair in range(2):
        for a in range(OPS_SRC):
            for b in range(sink):
                m, f = (a, b) if pair == 0 else (OPS_SRC + b, sink + a)
                zr = z_ref[m * ev : (m + 1) * ev, :ev]
                zi = z_ref[m * ev : (m + 1) * ev, ev:]
                fr, fi = phi_ref[f, :ev], phi_ref[f, ev:]
                for part in range(2):
                    whole = zr * fr - zi * fi if part == 0 else zr * fi + zi * fr
                    acc[a, (pair * sink + b) * 2 + part] = jnp.sum(whole.reshape(ev // 8, 8, ev), axis=0)
    lanes = lax.broadcasted_iota(jnp.int32, (rows, ev), 1)
    total = jnp.zeros((rows, ev), jnp.float32)
    for a in range(OPS_SRC):
        sums = jnp.sum(jnp.sum(acc[a], axis=1), axis=1, keepdims=True)
        total = jnp.where(lanes == a, sums, total)
    for b in range(sink):
        own_ref[b] = total[2 * b : 2 * b + 2, :OPS_SRC]
        other_ref[b] = total[2 * (sink + b) : 2 * (sink + b) + 2, :OPS_SRC]


def shards(perambulators, elementals, elem_place, op_lists):
    size = lax.axis_size("tm")
    half = size // 2
    me = lax.axis_index("tm")
    upper = (me >= half).astype(jnp.int32)
    across = [(source, (source + half) % size) for source in range(size)]

    def flip(value, bit):
        return lax.ppermute(value, "tm", [(source, source ^ bit) for source in range(size)])

    def spread(first):
        pieces, bit = [first], half // 2
        while bit:
            pieces += [flip(piece, bit) for piece in pieces]
            if len(pieces) > 8:
                pieces = [jnp.concatenate(pieces[at : at + 2]) for at in range(0, len(pieces), 2)]
            bit //= 2
        return pieces

    list_len = op_lists.shape[1]
    sink = list_len - OPS_SRC
    per_owner, _, ev, _ = elementals.shape
    order = perambulators.shape[2]
    spins = order // ev

    base = per_owner * 2 * ev
    digits = jnp.stack([op_lists // 256, op_lists % 256]).reshape(1, -1)
    digits = jnp.pad(digits.astype(jnp.bfloat16), ((0, 15), (0, ev - digits.shape[1])))
    block = jnp.concatenate([elementals.reshape(base, ev), digits])[None]
    far_block = lax.ppermute(block, "tm", across)
    pieces = spread(block) + spread(far_block)
    far_digits = far_block[0, base, : op_lists.size * 2].astype(jnp.int32).reshape(2, 2, list_len)
    other_list = far_digits[0] * 256 + far_digits[1]
    rows = perambulators.reshape(-1, 2, spins, ev, order)

    def sent(first, count):
        return lax.dynamic_slice(rows, (1 - upper, 0, first, 0, 0), (1, 2, count, ev, order))[0]

    mu_a = lax.ppermute(sent(0, spins - 1), "tm", across)
    mu_b = lax.ppermute(sent(spins - 1, 1), "tm", across)

    kept = lax.dynamic_index_in_dim(perambulators, upper, 0, keepdims=False)
    tau_t = kept.reshape(2, spins, ev, order).transpose(1, 3, 0, 2).reshape(spins, order, 2 * ev)
    ops = jnp.concatenate(
        [
            lax.dynamic_index_in_dim(op_lists, upper, 0, keepdims=False),
            lax.dynamic_index_in_dim(other_list, upper, 0, keepdims=False),
        ]
    )
    entries = (
        list(range(OPS_SRC))
        + list(range(list_len + OPS_SRC, 2 * list_len))
        + list(range(OPS_SRC, list_len))
        + list(range(list_len, list_len + OPS_SRC))
    )
    smem = pl.BlockSpec(memory_space=pltpu.SMEM)
    vmem = pl.BlockSpec(memory_space=pltpu.VMEM)
    anyspace = pl.BlockSpec(memory_space=pl.ANY)
    width = list_len * ev
    depth = 2 * order
    w, phi = pl.pallas_call(
        functools.partial(apply_kernel, per_owner=per_owner, half=half),
        out_shape=(
            jax.ShapeDtypeStruct((spins, width, depth), jnp.bfloat16),
            jax.ShapeDtypeStruct((list_len, 2 * ev, ev), jnp.float32),
        ),
        in_specs=[smem] * 4 + [vmem] + [anyspace] * len(pieces),
        out_specs=(vmem, vmem),
        scratch_shapes=[
            pltpu.VMEM((size, *block.shape[1:]), jnp.bfloat16),
            pltpu.SemaphoreType.DMA((len(pieces),)),
        ],
        compiler_params=pltpu.CompilerParams(vmem_limit_bytes=(20 << 20) + 2 * size * block.size),
        cost_estimate=pl.CostEstimate(
            flops=2 * spins * width * depth * 2 * ev, bytes_accessed=2 * spins * width * depth, transcendentals=0
        ),
        name="apply",
    )(jnp.array(entries, jnp.int32), ops, elem_place, me[None], tau_t, *pieces)
    z = pl.pallas_call(
        functools.partial(early_kernel, entries=list_len),
        out_shape=jax.ShapeDtypeStruct((width, 2 * ev), jnp.float32),
        grid=(spins - 1,),
        in_specs=[
            pl.BlockSpec((1, width, depth), lambda s: (s, 0, 0)),
            pl.BlockSpec((2, 1, ev, order), lambda s: (0, s, 0, 0)),
        ],
        out_specs=pl.BlockSpec((width, 2 * ev), lambda s: (0, 0)),
        compiler_params=pltpu.CompilerParams(vmem_limit_bytes=24 << 20),
        cost_estimate=pl.CostEstimate(
            flops=2 * (spins - 1) * width * depth * 2 * ev,
            bytes_accessed=2 * (spins - 1) * width * depth,
            transcendentals=0,
        ),
        name="early",
    )(w, mu_a)
    small = jax.ShapeDtypeStruct((sink, 2, OPS_SRC), jnp.float32)
    own, other = pl.pallas_call(
        functools.partial(late_kernel, entries=list_len),
        out_shape=(small, small),
        grid=(1,),
        in_specs=[
            pl.BlockSpec((1, width, depth), lambda s: (spins - 1, 0, 0)),
            pl.BlockSpec((2, 1, ev, order), lambda s: (0, 0, 0, 0)),
            pl.BlockSpec((width, 2 * ev), lambda s: (0, 0)),
            pl.BlockSpec((list_len, 2 * ev, ev), lambda s: (0, 0, 0)),
        ],
        out_specs=(vmem, vmem),
        scratch_shapes=[
            pltpu.VMEM((width, 2 * ev), jnp.float32),
            pltpu.VMEM((OPS_SRC, 4 * sink, 8, ev), jnp.float32),
        ],
        compiler_params=pltpu.CompilerParams(vmem_limit_bytes=24 << 20),
        cost_estimate=pl.CostEstimate(
            flops=2 * width * depth * 2 * ev, bytes_accessed=2 * width * depth, transcendentals=0
        ),
        name="late",
    )(w, mu_b, z, phi)
    back = lax.ppermute(other, "tm", across)
    both = jnp.where(upper == 0, jnp.stack([own, back]), jnp.stack([back, own]))
    return both.transpose(0, 2, 3, 1)


def solution(mesh):
    return jax.shard_map(
        shards,
        mesh=mesh,
        in_specs=(
            P(("cfg", "tm"), None, None, None),
            P(("cfg", "tm"), None, None, None),
            P("cfg"),
            P(("cfg", "tm"), None),
        ),
        out_specs=P(("cfg", "tm"), None, None, None),
        check_vma=False,
    )
```

```python
import functools

import jax
import jax.numpy as jnp
from jax import lax
from jax.experimental import pallas as pl
from jax.experimental.pallas import tpu as pltpu
from jax.sharding import PartitionSpec as P

OPS_SRC = 6
NT = (((1,), (1,)), ((), ()))


def apply_kernel(src, ops, place, self_id, tau_t, *refs, per_owner, half):
    *pieces, w_ref, phi_ref, table, sem = refs
    count = ops.shape[0]
    spins, order, twice = tau_t.shape
    ev = twice // 2
    steps = half.bit_length() - 1
    each = pieces[0].shape[0]
    copies = [
        pltpu.make_async_copy(piece, table.at[pl.ds(at * each, each)], sem.at[at]) for at, piece in enumerate(pieces)
    ]
    for copy in copies:
        copy.start()
    for copy in copies:
        copy.wait()

    def entry_of(slot):
        row = place[ops[src[slot]]]
        owner = lax.div(row, per_owner)
        apart = lax.bitwise_xor(owner, self_id[0])
        index = half * (apart >= half).astype(jnp.int32)
        for step in range(steps):
            bit = lax.bitwise_and(lax.shift_right_logical(apart, jnp.int32(steps - 1 - step)), 1)
            index = index + bit * (1 << step)
        return table[index, pl.ds(pl.multiple_of((row - owner * per_owner) * twice, twice), twice)]

    def product(m, _):
        phi = entry_of(m)
        real, imag = phi[:ev], phi[ev:]
        lifted = jnp.concatenate(
            [jnp.concatenate([real, -imag], axis=1), jnp.concatenate([imag, real], axis=1)], axis=0
        )
        row = pl.multiple_of(m * ev, ev)
        for inner in range(spins):
            out = lax.dot_general(tau_t[inner], lifted, NT, preferred_element_type=jnp.float32)
            out = out.astype(jnp.bfloat16)
            for outer in range(spins):
                w_ref[outer, pl.ds(row, ev), inner * twice : (inner + 1) * twice] = out[
                    outer * ev : (outer + 1) * ev
                ]
        return 0

    lax.fori_loop(0, count // 2, product, 0)

    def keep(m, _):
        phi_ref[m] = entry_of(count // 2 + m).astype(jnp.float32)
        return 0

    lax.fori_loop(0, count // 2, keep, 0)


def lift_rows(mu, spins):
    ev = mu.shape[1]
    top, low = [], []
    for inner in range(spins):
        real = mu[0, :, inner * ev : (inner + 1) * ev]
        imag = mu[1, :, inner * ev : (inner + 1) * ev]
        top += [real, -imag]
        low += [imag, real]
    return jnp.concatenate([jnp.concatenate(top, axis=1), jnp.concatenate(low, axis=1)], axis=0)


def last_kernel(w_ref, mu_ref, phi_ref, own_ref, other_ref, acc, *, entries):
    spins, _, depth = w_ref.shape
    ev = mu_ref.shape[2]
    sink = entries - OPS_SRC
    lifted = [lift_rows(mu_ref[:, s], spins) for s in range(spins)]
    for first in range(0, entries, 4):
        block = range(first, min(first + 4, entries))
        rows = slice(first * ev, (block[-1] + 1) * ev)
        z = lax.dot_general(w_ref[0, rows], lifted[0], NT, preferred_element_type=jnp.float32)
        for s in range(1, spins):
            z = z + lax.dot_general(w_ref[s, rows], lifted[s], NT, preferred_element_type=jnp.float32)
        for m in block:
            at = (m - first) * ev
            zr, zi = z[at : at + ev, :ev], z[at : at + ev, ev:]
            if m < OPS_SRC:
                spots = [(b, m, b) for b in range(sink)]
            else:
                spots = [(sink + a, a, m - OPS_SRC + sink) for a in range(OPS_SRC)]
            for f, a, row in spots:
                fr, fi = phi_ref[f, :ev], phi_ref[f, ev:]
                acc[a, 2 * row] = jnp.sum((zr * fr - zi * fi).reshape(ev // 8, 8, ev), axis=0)
                acc[a, 2 * row + 1] = jnp.sum((zr * fi + zi * fr).reshape(ev // 8, 8, ev), axis=0)
    lanes = lax.broadcasted_iota(jnp.int32, (4 * sink, ev), 1)
    total = jnp.zeros((4 * sink, ev), jnp.float32)
    for a in range(OPS_SRC):
        sums = jnp.sum(jnp.sum(acc[a], axis=1), axis=1, keepdims=True)
        total = jnp.where(lanes == a, sums, total)
    for b in range(sink):
        own_ref[b] = total[2 * b : 2 * b + 2, :OPS_SRC]
        other_ref[b] = total[2 * (sink + b) : 2 * (sink + b) + 2, :OPS_SRC]


def pack_kernel(elem_ref, list_ref, block_ref, digits, narrow, sem):
    base = elem_ref.shape[0]
    pairs, list_len = list_ref.shape
    body = pltpu.make_async_copy(elem_ref, block_ref.at[0, pl.ds(0, base)], sem.at[0])
    body.start()
    lists = list_ref[...]
    digits[...] = jnp.zeros_like(digits)
    digits[:pairs, :list_len] = lax.shift_right_logical(lists, 8).astype(jnp.float32)
    digits[8 : 8 + pairs, :list_len] = lax.bitwise_and(lists, 255).astype(jnp.float32)
    narrow[...] = digits[...].astype(jnp.bfloat16)
    tail = pltpu.make_async_copy(narrow, block_ref.at[0, pl.ds(base, 16)], sem.at[1])
    tail.start()
    tail.wait()
    body.wait()


def shards(perambulators, elementals, elem_place, op_lists):
    size = lax.axis_size("tm")
    half = size // 2
    me = lax.axis_index("tm")
    upper = (me >= half).astype(jnp.int32)
    across = [(source, (source + half) % size) for source in range(size)]

    def flip(value, bit):
        return lax.ppermute(value, "tm", [(source, source ^ bit) for source in range(size)])

    def spread(first):
        pieces, bit = [first], half // 2
        while bit:
            pieces += [flip(piece, bit) for piece in pieces]
            if len(pieces) > 8:
                pieces = [jnp.concatenate(pieces[at : at + 2]) for at in range(0, len(pieces), 2)]
            bit //= 2
        return pieces

    list_len = op_lists.shape[1]
    sink = list_len - OPS_SRC
    per_owner, _, ev, _ = elementals.shape
    order = perambulators.shape[2]
    spins = order // ev

    base = per_owner * 2 * ev
    block = pl.pallas_call(
        pack_kernel,
        out_shape=jax.ShapeDtypeStruct((1, base + 16, ev), jnp.bfloat16),
        in_specs=[pl.BlockSpec(memory_space=pl.ANY), pl.BlockSpec(memory_space=pltpu.VMEM)],
        out_specs=pl.BlockSpec(memory_space=pl.ANY),
        scratch_shapes=[
            pltpu.VMEM((16, ev), jnp.float32),
            pltpu.VMEM((16, ev), jnp.bfloat16),
            pltpu.SemaphoreType.DMA((2,)),
        ],
        compiler_params=pltpu.CompilerParams(vmem_limit_bytes=1 << 20),
        name="pack",
    )(elementals.reshape(base, ev), op_lists)
    far_block = lax.ppermute(block, "tm", across)
    pieces = spread(block) + spread(far_block)
    far_digits = far_block[0, base:].astype(jnp.int32)
    pairs = op_lists.shape[0]
    other_list = far_digits[:pairs, :list_len] * 256 + far_digits[8 : 8 + pairs, :list_len]
    rows = perambulators.reshape(-1, 2, spins, ev, order)

    def sent(first, count):
        return lax.dynamic_slice(rows, (1 - upper, 0, first, 0, 0), (1, 2, count, ev, order))[0]

    mu = lax.ppermute(sent(0, spins), "tm", across)

    kept = lax.dynamic_index_in_dim(perambulators, upper, 0, keepdims=False)
    tau_t = kept.reshape(2, spins, ev, order).transpose(1, 3, 0, 2).reshape(spins, order, 2 * ev)
    ops = jnp.concatenate(
        [
            lax.dynamic_index_in_dim(op_lists, upper, 0, keepdims=False),
            lax.dynamic_index_in_dim(other_list, upper, 0, keepdims=False),
        ]
    )
    entries = (
        list(range(OPS_SRC))
        + list(range(list_len + OPS_SRC, 2 * list_len))
        + list(range(OPS_SRC, list_len))
        + list(range(list_len, list_len + OPS_SRC))
    )
    smem = pl.BlockSpec(memory_space=pltpu.SMEM)
    vmem = pl.BlockSpec(memory_space=pltpu.VMEM)
    anyspace = pl.BlockSpec(memory_space=pl.ANY)
    width = list_len * ev
    depth = 2 * order
    w, phi = pl.pallas_call(
        functools.partial(apply_kernel, per_owner=per_owner, half=half),
        out_shape=(
            jax.ShapeDtypeStruct((spins, width, depth), jnp.bfloat16),
            jax.ShapeDtypeStruct((list_len, 2 * ev, ev), jnp.float32),
        ),
        in_specs=[smem] * 4 + [vmem] + [anyspace] * len(pieces),
        out_specs=(vmem, vmem),
        scratch_shapes=[
            pltpu.VMEM((size, *block.shape[1:]), jnp.bfloat16),
            pltpu.SemaphoreType.DMA((len(pieces),)),
        ],
        compiler_params=pltpu.CompilerParams(vmem_limit_bytes=(20 << 20) + 2 * size * block.size),
        cost_estimate=pl.CostEstimate(
            flops=2 * spins * width * depth * 2 * ev, bytes_accessed=2 * spins * width * depth, transcendentals=0
        ),
        name="apply",
    )(jnp.array(entries, jnp.int32), ops, elem_place, me[None], tau_t, *pieces)
    small = jax.ShapeDtypeStruct((sink, 2, OPS_SRC), jnp.float32)
    own, other = pl.pallas_call(
        functools.partial(last_kernel, entries=list_len),
        out_shape=(small, small),
        in_specs=[vmem] * 3,
        out_specs=(vmem, vmem),
        scratch_shapes=[pltpu.VMEM((OPS_SRC, 4 * sink, 8, ev), jnp.float32)],
        compiler_params=pltpu.CompilerParams(vmem_limit_bytes=20 << 20),
        cost_estimate=pl.CostEstimate(
            flops=2 * spins * width * depth * 2 * ev, bytes_accessed=2 * spins * width * depth, transcendentals=0
        ),
        name="last",
    )(w, mu, phi)
    back = lax.ppermute(other, "tm", across)
    both = jnp.where(upper == 0, jnp.stack([own, back]), jnp.stack([back, own]))
    return both.transpose(0, 2, 3, 1)


def solution(mesh):
    return jax.shard_map(
        shards,
        mesh=mesh,
        in_specs=(
            P(("cfg", "tm"), None, None, None),
            P(("cfg", "tm"), None, None, None),
            P("cfg"),
            P(("cfg", "tm"), None),
        ),
        out_specs=P(("cfg", "tm"), None, None, None),
        check_vma=False,
    )
```

```python
import functools

import jax
import jax.numpy as jnp
from jax import lax
from jax.experimental import pallas as pl
from jax.experimental.pallas import tpu as pltpu
from jax.sharding import PartitionSpec as P

OPS_SRC = 6
NT = (((1,), (1,)), ((), ()))


def apply_kernel(src, ops, place, self_id, tau_t, *refs, per_owner, half):
    *pieces, w_ref, phi_ref, table, sem = refs
    count = ops.shape[0]
    spins, order, twice = tau_t.shape
    ev = twice // 2
    steps = half.bit_length() - 1
    each = pieces[0].shape[0]
    copies = [
        pltpu.make_async_copy(piece, table.at[pl.ds(at * each, each)], sem.at[at]) for at, piece in enumerate(pieces)
    ]
    for copy in copies:
        copy.start()
    for copy in copies:
        copy.wait()

    def entry_of(slot):
        row = place[ops[src[slot]]]
        owner = lax.div(row, per_owner)
        apart = lax.bitwise_xor(owner, self_id[0])
        index = half * (apart >= half).astype(jnp.int32)
        for step in range(steps):
            bit = lax.bitwise_and(lax.shift_right_logical(apart, jnp.int32(steps - 1 - step)), 1)
            index = index + bit * (1 << step)
        return table[index, pl.ds(pl.multiple_of((row - owner * per_owner) * twice, twice), twice)]

    def product(m, _):
        phi = entry_of(m)
        real, imag = phi[:ev], phi[ev:]
        lifted = jnp.concatenate(
            [jnp.concatenate([real, -imag], axis=1), jnp.concatenate([imag, real], axis=1)], axis=0
        )
        row = pl.multiple_of(m * ev, ev)
        for inner in range(spins):
            out = lax.dot_general(tau_t[inner], lifted, NT, preferred_element_type=jnp.float32)
            out = out.astype(jnp.bfloat16)
            for outer in range(spins):
                w_ref[outer, pl.ds(row, ev), inner * twice : (inner + 1) * twice] = out[
                    outer * ev : (outer + 1) * ev
                ]
        return 0

    lax.fori_loop(0, count // 2, product, 0)

    def keep(m, _):
        phi_ref[m] = entry_of(count // 2 + m).astype(jnp.float32)
        return 0

    lax.fori_loop(0, count // 2, keep, 0)


def lift_rows(mu, spins):
    ev = mu.shape[1]
    top, low = [], []
    for inner in range(spins):
        real = mu[0, :, inner * ev : (inner + 1) * ev]
        imag = mu[1, :, inner * ev : (inner + 1) * ev]
        top += [real, -imag]
        low += [imag, real]
    return jnp.concatenate([jnp.concatenate(top, axis=1), jnp.concatenate(low, axis=1)], axis=0)


def last_kernel(w_ref, mu_ref, phi_ref, own_ref, other_ref, acc, *, entries):
    spins, _, depth = w_ref.shape
    ev = mu_ref.shape[2]
    sink = entries - OPS_SRC
    lifted = [lift_rows(mu_ref[:, s], spins) for s in range(spins)]
    for first in range(0, entries, 4):
        block = range(first, min(first + 4, entries))
        rows = slice(first * ev, (block[-1] + 1) * ev)
        z = lax.dot_general(w_ref[0, rows], lifted[0], NT, preferred_element_type=jnp.float32)
        for s in range(1, spins):
            z = z + lax.dot_general(w_ref[s, rows], lifted[s], NT, preferred_element_type=jnp.float32)
        for m in block:
            at = (m - first) * ev
            zr, zi = z[at : at + ev, :ev], z[at : at + ev, ev:]
            if m < OPS_SRC:
                spots = [(b, m, b) for b in range(sink)]
            else:
                spots = [(sink + a, a, m - OPS_SRC + sink) for a in range(OPS_SRC)]
            for f, a, row in spots:
                fr, fi = phi_ref[f, :ev], phi_ref[f, ev:]
                acc[a, 2 * row] = jnp.sum((zr * fr - zi * fi).reshape(ev // 8, 8, ev), axis=0)
                acc[a, 2 * row + 1] = jnp.sum((zr * fi + zi * fr).reshape(ev // 8, 8, ev), axis=0)
    lanes = lax.broadcasted_iota(jnp.int32, (4 * sink, ev), 1)
    total = jnp.zeros((4 * sink, ev), jnp.float32)
    for a in range(OPS_SRC):
        sums = jnp.sum(jnp.sum(acc[a], axis=1), axis=1, keepdims=True)
        total = jnp.where(lanes == a, sums, total)
    for b in range(sink):
        own_ref[b] = total[2 * b : 2 * b + 2, :OPS_SRC]
        other_ref[b] = total[2 * (sink + b) : 2 * (sink + b) + 2, :OPS_SRC]


def pack_kernel(elem_ref, list_ref, block_ref, digits, narrow, sem):
    base = elem_ref.shape[0]
    pairs, list_len = list_ref.shape
    body = pltpu.make_async_copy(elem_ref, block_ref.at[0, pl.ds(0, base)], sem.at[0])
    body.start()
    lists = list_ref[...]
    digits[...] = jnp.zeros_like(digits)
    digits[:pairs, :list_len] = lax.shift_right_logical(lists, 8).astype(jnp.float32)
    digits[8 : 8 + pairs, :list_len] = lax.bitwise_and(lists, 255).astype(jnp.float32)
    narrow[...] = digits[...].astype(jnp.bfloat16)
    tail = pltpu.make_async_copy(narrow, block_ref.at[0, pl.ds(base, 16)], sem.at[1])
    tail.start()
    tail.wait()
    body.wait()


def shards(perambulators, elementals, elem_place, op_lists):
    size = lax.axis_size("tm")
    half = size // 2
    me = lax.axis_index("tm")
    upper = (me >= half).astype(jnp.int32)
    across = [(source, (source + half) % size) for source in range(size)]

    def flip(value, bit):
        return lax.ppermute(value, "tm", [(source, source ^ bit) for source in range(size)])

    def spread(first):
        pieces, bit = [first], half // 2
        while bit:
            pieces += [flip(piece, bit) for piece in pieces]
            if len(pieces) > 8:
                pieces = [jnp.concatenate(pieces[at : at + 2]) for at in range(0, len(pieces), 2)]
            bit //= 2
        return pieces

    list_len = op_lists.shape[1]
    sink = list_len - OPS_SRC
    per_owner, _, ev, _ = elementals.shape
    order = perambulators.shape[2]
    spins = order // ev

    base = per_owner * 2 * ev
    block = pl.pallas_call(
        pack_kernel,
        out_shape=jax.ShapeDtypeStruct((1, base + 16, ev), jnp.bfloat16),
        in_specs=[pl.BlockSpec(memory_space=pl.ANY), pl.BlockSpec(memory_space=pltpu.VMEM)],
        out_specs=pl.BlockSpec(memory_space=pl.ANY),
        scratch_shapes=[
            pltpu.VMEM((16, ev), jnp.float32),
            pltpu.VMEM((16, ev), jnp.bfloat16),
            pltpu.SemaphoreType.DMA((2,)),
        ],
        compiler_params=pltpu.CompilerParams(vmem_limit_bytes=1 << 20),
        name="pack",
    )(elementals.reshape(base, ev), op_lists)
    far_block = lax.ppermute(block, "tm", across)
    pieces = spread(block) + spread(far_block)
    far_digits = far_block[0, base:].astype(jnp.int32)
    pairs = op_lists.shape[0]
    other_list = far_digits[:pairs, :list_len] * 256 + far_digits[8 : 8 + pairs, :list_len]
    kept = lax.dynamic_index_in_dim(perambulators, upper, 0, keepdims=False)
    tau_t = kept.reshape(2, spins, ev, order).transpose(1, 3, 0, 2).reshape(spins, order, 2 * ev)
    tau_t, held = lax.optimization_barrier((tau_t, perambulators))
    rows = held.reshape(-1, 2, spins, ev, order)

    def sent(first, count):
        return lax.dynamic_slice(rows, (1 - upper, 0, first, 0, 0), (1, 2, count, ev, order))[0]

    mu = lax.ppermute(sent(0, spins), "tm", across)

    ops = jnp.concatenate(
        [
            lax.dynamic_index_in_dim(op_lists, upper, 0, keepdims=False),
            lax.dynamic_index_in_dim(other_list, upper, 0, keepdims=False),
        ]
    )
    entries = (
        list(range(OPS_SRC))
        + list(range(list_len + OPS_SRC, 2 * list_len))
        + list(range(OPS_SRC, list_len))
        + list(range(list_len, list_len + OPS_SRC))
    )
    smem = pl.BlockSpec(memory_space=pltpu.SMEM)
    vmem = pl.BlockSpec(memory_space=pltpu.VMEM)
    anyspace = pl.BlockSpec(memory_space=pl.ANY)
    width = list_len * ev
    depth = 2 * order
    w, phi = pl.pallas_call(
        functools.partial(apply_kernel, per_owner=per_owner, half=half),
        out_shape=(
            jax.ShapeDtypeStruct((spins, width, depth), jnp.bfloat16),
            jax.ShapeDtypeStruct((list_len, 2 * ev, ev), jnp.float32),
        ),
        in_specs=[smem] * 4 + [vmem] + [anyspace] * len(pieces),
        out_specs=(vmem, vmem),
        scratch_shapes=[
            pltpu.VMEM((size, *block.shape[1:]), jnp.bfloat16),
            pltpu.SemaphoreType.DMA((len(pieces),)),
        ],
        compiler_params=pltpu.CompilerParams(vmem_limit_bytes=(20 << 20) + 2 * size * block.size),
        cost_estimate=pl.CostEstimate(
            flops=2 * spins * width * depth * 2 * ev, bytes_accessed=2 * spins * width * depth, transcendentals=0
        ),
        name="apply",
    )(jnp.array(entries, jnp.int32), ops, elem_place, me[None], tau_t, *pieces)
    small = jax.ShapeDtypeStruct((sink, 2, OPS_SRC), jnp.float32)
    own, other = pl.pallas_call(
        functools.partial(last_kernel, entries=list_len),
        out_shape=(small, small),
        in_specs=[vmem] * 3,
        out_specs=(vmem, vmem),
        scratch_shapes=[pltpu.VMEM((OPS_SRC, 4 * sink, 8, ev), jnp.float32)],
        compiler_params=pltpu.CompilerParams(vmem_limit_bytes=20 << 20),
        cost_estimate=pl.CostEstimate(
            flops=2 * spins * width * depth * 2 * ev, bytes_accessed=2 * spins * width * depth, transcendentals=0
        ),
        name="last",
    )(w, mu, phi)
    back = lax.ppermute(other, "tm", across)
    both = jnp.where(upper == 0, jnp.stack([own, back]), jnp.stack([back, own]))
    return both.transpose(0, 2, 3, 1)


def solution(mesh):
    return jax.shard_map(
        shards,
        mesh=mesh,
        in_specs=(
            P(("cfg", "tm"), None, None, None),
            P(("cfg", "tm"), None, None, None),
            P("cfg"),
            P(("cfg", "tm"), None),
        ),
        out_specs=P(("cfg", "tm"), None, None, None),
        check_vma=False,
    )
```

```python
import functools

import jax
import jax.numpy as jnp
from jax import lax
from jax.experimental import pallas as pl
from jax.experimental.pallas import tpu as pltpu
from jax.sharding import PartitionSpec as P

OPS_SRC = 6
NT = (((1,), (1,)), ((), ()))


def apply_kernel(src, ops, place, self_id, tau_t, *refs, per_owner, half):
    *pieces, w_ref, phi_ref, buf, sem = refs
    count = ops.shape[0]
    spins, order, twice = tau_t.shape
    ev = twice // 2
    steps = half.bit_length() - 1
    each = pieces[0].shape[0]

    def fetch(slot, _):
        row = place[ops[src[slot]]]
        owner = lax.div(row, per_owner)
        apart = lax.bitwise_xor(owner, self_id[0])
        index = half * (apart >= half).astype(jnp.int32)
        for step in range(steps):
            bit = lax.bitwise_and(lax.shift_right_logical(apart, jnp.int32(steps - 1 - step)), 1)
            index = index + bit * (1 << step)
        start = pl.multiple_of((row - owner * per_owner) * twice, twice)
        which = lax.div(index, each)

        def choose(low, high):
            if high - low == 1:
                source = pieces[low].at[index - low * each, pl.ds(start, twice)]
                pltpu.make_async_copy(source, buf.at[slot], sem.at[slot]).start()
                return
            middle = (low + high) // 2
            pl.when(which < middle)(functools.partial(choose, low, middle))
            pl.when(which >= middle)(functools.partial(choose, middle, high))

        choose(0, len(pieces))
        return 0

    def arrive(slot):
        pltpu.make_async_copy(pieces[0].at[0, pl.ds(0, twice)], buf.at[slot], sem.at[slot]).wait()

    lax.fori_loop(0, count, fetch, 0)
    for m in range(count // 2):
        arrive(m)
    for m in range(count // 2):
        real, imag = buf[m, :ev], buf[m, ev:]
        lifted = jnp.concatenate(
            [jnp.concatenate([real, -imag], axis=1), jnp.concatenate([imag, real], axis=1)], axis=0
        )
        for inner in range(spins):
            out = lax.dot_general(tau_t[inner], lifted, NT, preferred_element_type=jnp.float32)
            out = out.astype(jnp.bfloat16)
            for outer in range(spins):
                w_ref[outer, m * ev : (m + 1) * ev, inner * twice : (inner + 1) * twice] = out[
                    outer * ev : (outer + 1) * ev
                ]
    for m in range(count // 2, count):
        arrive(m)
        phi_ref[m - count // 2] = buf[m].astype(jnp.float32)


def lift_rows(mu, spins):
    ev = mu.shape[1]
    top, low = [], []
    for inner in range(spins):
        real = mu[0, :, inner * ev : (inner + 1) * ev]
        imag = mu[1, :, inner * ev : (inner + 1) * ev]
        top += [real, -imag]
        low += [imag, real]
    return jnp.concatenate([jnp.concatenate(top, axis=1), jnp.concatenate(low, axis=1)], axis=0)


def products(w_ref, mu_ref, first, rows):
    spins = w_ref.shape[0]
    total = None
    for s in range(mu_ref.shape[1]):
        lifted = lift_rows(mu_ref[:, s], spins)
        part = lax.dot_general(w_ref[first + s, rows], lifted, NT, preferred_element_type=jnp.float32)
        total = part if total is None else total + part
    return total


def early_kernel(w_ref, mu_ref, z_ref, *, ev):
    height = z_ref.shape[0]
    for at in range(0, height, 4 * ev):
        rows = slice(at, min(at + 4 * ev, height))
        z_ref[rows] = products(w_ref, mu_ref, 0, rows)


def last_kernel(w_ref, mu_ref, z_ref, phi_ref, own_ref, other_ref, acc, *, entries, first_spin):
    ev = mu_ref.shape[2]
    sink = entries - OPS_SRC
    for first in range(0, entries, 4):
        block = range(first, min(first + 4, entries))
        rows = slice(first * ev, (block[-1] + 1) * ev)
        z = z_ref[rows] + products(w_ref, mu_ref, first_spin, rows)
        for m in block:
            at = (m - first) * ev
            zr, zi = z[at : at + ev, :ev], z[at : at + ev, ev:]
            if m < OPS_SRC:
                spots = [(b, m, b) for b in range(sink)]
            else:
                spots = [(sink + a, a, m - OPS_SRC + sink) for a in range(OPS_SRC)]
            for f, a, row in spots:
                fr, fi = phi_ref[f, :ev], phi_ref[f, ev:]
                acc[a, 2 * row] = jnp.sum((zr * fr - zi * fi).reshape(ev // 8, 8, ev), axis=0)
                acc[a, 2 * row + 1] = jnp.sum((zr * fi + zi * fr).reshape(ev // 8, 8, ev), axis=0)
    lanes = lax.broadcasted_iota(jnp.int32, (4 * sink, ev), 1)
    total = jnp.zeros((4 * sink, ev), jnp.float32)
    for a in range(OPS_SRC):
        sums = jnp.sum(jnp.sum(acc[a], axis=1), axis=1, keepdims=True)
        total = jnp.where(lanes == a, sums, total)
    for b in range(sink):
        own_ref[b] = total[2 * b : 2 * b + 2, :OPS_SRC]
        other_ref[b] = total[2 * (sink + b) : 2 * (sink + b) + 2, :OPS_SRC]


def pack_kernel(elem_ref, list_ref, block_ref, digits, narrow, sem):
    base = elem_ref.shape[0]
    pairs, list_len = list_ref.shape
    body = pltpu.make_async_copy(elem_ref, block_ref.at[0, pl.ds(0, base)], sem.at[0])
    body.start()
    lists = list_ref[...]
    digits[...] = jnp.zeros_like(digits)
    digits[:pairs, :list_len] = lax.shift_right_logical(lists, 8).astype(jnp.float32)
    digits[8 : 8 + pairs, :list_len] = lax.bitwise_and(lists, 255).astype(jnp.float32)
    narrow[...] = digits[...].astype(jnp.bfloat16)
    tail = pltpu.make_async_copy(narrow, block_ref.at[0, pl.ds(base, 16)], sem.at[1])
    tail.start()
    tail.wait()
    body.wait()


def shards(perambulators, elementals, elem_place, op_lists):
    size = lax.axis_size("tm")
    half = size // 2
    me = lax.axis_index("tm")
    upper = (me >= half).astype(jnp.int32)
    across = [(source, (source + half) % size) for source in range(size)]

    def flip(value, bit):
        return lax.ppermute(value, "tm", [(source, source ^ bit) for source in range(size)])

    def spread(first):
        pieces, bit = [first], half // 2
        while bit:
            pieces += [flip(piece, bit) for piece in pieces]
            if len(pieces) > 8:
                pieces = [jnp.concatenate(pieces[at : at + 2]) for at in range(0, len(pieces), 2)]
            bit //= 2
        return pieces

    list_len = op_lists.shape[1]
    sink = list_len - OPS_SRC
    per_owner, _, ev, _ = elementals.shape
    order = perambulators.shape[2]
    spins = order // ev

    base = per_owner * 2 * ev
    block = pl.pallas_call(
        pack_kernel,
        out_shape=jax.ShapeDtypeStruct((1, base + 16, ev), jnp.bfloat16),
        in_specs=[pl.BlockSpec(memory_space=pl.ANY), pl.BlockSpec(memory_space=pltpu.VMEM)],
        out_specs=pl.BlockSpec(memory_space=pl.ANY),
        scratch_shapes=[
            pltpu.VMEM((16, ev), jnp.float32),
            pltpu.VMEM((16, ev), jnp.bfloat16),
            pltpu.SemaphoreType.DMA((2,)),
        ],
        compiler_params=pltpu.CompilerParams(vmem_limit_bytes=1 << 20),
        name="pack",
    )(elementals.reshape(base, ev), op_lists)
    far_block = lax.ppermute(block, "tm", across)
    pieces = spread(block) + spread(far_block)
    far_digits = far_block[0, base:].astype(jnp.int32)
    pairs = op_lists.shape[0]
    other_list = far_digits[:pairs, :list_len] * 256 + far_digits[8 : 8 + pairs, :list_len]
    kept = lax.dynamic_index_in_dim(perambulators, upper, 0, keepdims=False)
    tau_t = kept.reshape(2, spins, ev, order).transpose(1, 3, 0, 2).reshape(spins, order, 2 * ev)
    tau_t, held = lax.optimization_barrier((tau_t, perambulators))
    rows = held.reshape(-1, 2, spins, ev, order)
    split = spins - 1

    def sent(first, count):
        return lax.dynamic_slice(rows, (1 - upper, 0, first, 0, 0), (1, 2, count, ev, order))[0]

    mu_a = lax.ppermute(sent(0, split), "tm", across)
    mu_b = lax.ppermute(sent(split, spins - split), "tm", across)

    ops = jnp.concatenate(
        [
            lax.dynamic_index_in_dim(op_lists, upper, 0, keepdims=False),
            lax.dynamic_index_in_dim(other_list, upper, 0, keepdims=False),
        ]
    )
    entries = (
        list(range(OPS_SRC))
        + list(range(list_len + OPS_SRC, 2 * list_len))
        + list(range(OPS_SRC, list_len))
        + list(range(list_len, list_len + OPS_SRC))
    )
    smem = pl.BlockSpec(memory_space=pltpu.SMEM)
    vmem = pl.BlockSpec(memory_space=pltpu.VMEM)
    anyspace = pl.BlockSpec(memory_space=pl.ANY)
    width = list_len * ev
    depth = 2 * order
    w, phi = pl.pallas_call(
        functools.partial(apply_kernel, per_owner=per_owner, half=half),
        out_shape=(
            jax.ShapeDtypeStruct((spins, width, depth), jnp.bfloat16),
            jax.ShapeDtypeStruct((list_len, 2 * ev, ev), jnp.float32),
        ),
        in_specs=[smem] * 4 + [vmem] + [anyspace] * len(pieces),
        out_specs=(vmem, vmem),
        scratch_shapes=[
            pltpu.VMEM((2 * list_len, 2 * ev, ev), jnp.bfloat16),
            pltpu.SemaphoreType.DMA((2 * list_len,)),
        ],
        compiler_params=pltpu.CompilerParams(vmem_limit_bytes=24 << 20),
        cost_estimate=pl.CostEstimate(
            flops=2 * spins * width * depth * 2 * ev, bytes_accessed=2 * spins * width * depth, transcendentals=0
        ),
        name="apply",
    )(jnp.array(entries, jnp.int32), ops, elem_place, me[None], tau_t, *pieces)
    z = pl.pallas_call(
        functools.partial(early_kernel, ev=ev),
        out_shape=jax.ShapeDtypeStruct((width, 2 * ev), jnp.float32),
        in_specs=[vmem] * 2,
        out_specs=vmem,
        compiler_params=pltpu.CompilerParams(vmem_limit_bytes=20 << 20),
        cost_estimate=pl.CostEstimate(
            flops=2 * spins * width * depth * 2 * ev, bytes_accessed=2 * spins * width * depth, transcendentals=0
        ),
        name="early",
    )(w, mu_a)
    small = jax.ShapeDtypeStruct((sink, 2, OPS_SRC), jnp.float32)
    own, other = pl.pallas_call(
        functools.partial(last_kernel, entries=list_len, first_spin=split),
        out_shape=(small, small),
        in_specs=[vmem] * 4,
        out_specs=(vmem, vmem),
        scratch_shapes=[pltpu.VMEM((OPS_SRC, 4 * sink, 8, ev), jnp.float32)],
        compiler_params=pltpu.CompilerParams(vmem_limit_bytes=20 << 20),
        cost_estimate=pl.CostEstimate(flops=2 * width * depth * ev, bytes_accessed=8 * width * ev, transcendentals=0),
        name="last",
    )(w, mu_b, z, phi)
    back = lax.ppermute(other, "tm", across)
    both = jnp.where(upper == 0, jnp.stack([own, back]), jnp.stack([back, own]))
    return both.transpose(0, 2, 3, 1)


def solution(mesh):
    return jax.shard_map(
        shards,
        mesh=mesh,
        in_specs=(
            P(("cfg", "tm"), None, None, None),
            P(("cfg", "tm"), None, None, None),
            P("cfg"),
            P(("cfg", "tm"), None),
        ),
        out_specs=P(("cfg", "tm"), None, None, None),
        check_vma=False,
    )
```

```python
import functools

import jax
import jax.numpy as jnp
from jax import lax
from jax.experimental import pallas as pl
from jax.experimental.pallas import tpu as pltpu
from jax.sharding import PartitionSpec as P

OPS_SRC = 6
NT = (((1,), (1,)), ((), ()))


def apply_kernel(src, ops, place, self_id, tau_t, *refs, per_owner, half):
    *pieces, w_ref, phi_ref, buf, sem = refs
    count = ops.shape[0]
    spins, order, twice = tau_t.shape
    ev = twice // 2
    steps = half.bit_length() - 1
    each = pieces[0].shape[0]

    def fetch(slot, _):
        row = place[ops[src[slot]]]
        owner = lax.div(row, per_owner)
        apart = lax.bitwise_xor(owner, self_id[0])
        index = half * (apart >= half).astype(jnp.int32)
        for step in range(steps):
            bit = lax.bitwise_and(lax.shift_right_logical(apart, jnp.int32(steps - 1 - step)), 1)
            index = index + bit * (1 << step)
        start = pl.multiple_of((row - owner * per_owner) * twice, twice)
        which = lax.div(index, each)

        def choose(low, high):
            if high - low == 1:
                source = pieces[low].at[index - low * each, pl.ds(start, twice)]
                pltpu.make_async_copy(source, buf.at[slot], sem.at[slot]).start()
                return
            middle = (low + high) // 2
            pl.when(which < middle)(functools.partial(choose, low, middle))
            pl.when(which >= middle)(functools.partial(choose, middle, high))

        choose(0, len(pieces))
        return 0

    def arrive(slot):
        pltpu.make_async_copy(pieces[0].at[0, pl.ds(0, twice)], buf.at[slot], sem.at[slot]).wait()

    lax.fori_loop(0, count, fetch, 0)
    for m in range(count // 2):
        arrive(m)
    for m in range(count // 2):
        real, imag = buf[m, :ev], buf[m, ev:]
        lifted = jnp.concatenate(
            [jnp.concatenate([real, -imag], axis=1), jnp.concatenate([imag, real], axis=1)], axis=0
        )
        for inner in range(spins):
            out = lax.dot_general(tau_t[inner], lifted, NT, preferred_element_type=jnp.float32)
            out = out.astype(jnp.bfloat16)
            for outer in range(spins):
                w_ref[outer, m * ev : (m + 1) * ev, inner * twice : (inner + 1) * twice] = out[
                    outer * ev : (outer + 1) * ev
                ]
    for m in range(count // 2, count):
        arrive(m)
        real, imag = buf[m, :ev].astype(jnp.float32), buf[m, ev:].astype(jnp.float32)
        phi_ref[m - count // 2, :ev] = real
        phi_ref[m - count // 2, ev : 2 * ev] = imag - real
        phi_ref[m - count // 2, 2 * ev :] = real + imag


def lift_rows(mu, spins):
    ev = mu.shape[1]
    top, low = [], []
    for inner in range(spins):
        real = mu[0, :, inner * ev : (inner + 1) * ev]
        imag = mu[1, :, inner * ev : (inner + 1) * ev]
        top += [real, -imag]
        low += [imag, real]
    return jnp.concatenate([jnp.concatenate(top, axis=1), jnp.concatenate(low, axis=1)], axis=0)


def products(w_ref, mu_ref, first, rows):
    spins = w_ref.shape[0]
    total = None
    for s in range(mu_ref.shape[1]):
        lifted = lift_rows(mu_ref[:, s], spins)
        part = lax.dot_general(w_ref[first + s, rows], lifted, NT, preferred_element_type=jnp.float32)
        total = part if total is None else total + part
    return total


def early_kernel(w_ref, mu_ref, z_ref, *, ev):
    height = z_ref.shape[0]
    for at in range(0, height, 4 * ev):
        rows = slice(at, min(at + 4 * ev, height))
        z_ref[rows] = products(w_ref, mu_ref, 0, rows)


def last_kernel(w_ref, mu_ref, z_ref, phi_ref, own_ref, other_ref, acc, *, entries, first_spin):
    ev = mu_ref.shape[2]
    sink = entries - OPS_SRC
    for first in range(0, entries, 4):
        block = range(first, min(first + 4, entries))
        rows = slice(first * ev, (block[-1] + 1) * ev)
        z = z_ref[rows] + products(w_ref, mu_ref, first_spin, rows)
        for m in block:
            at = (m - first) * ev
            zr, zi = z[at : at + ev, :ev], z[at : at + ev, ev:]
            both = zr + zi
            if m < OPS_SRC:
                spots = [(b, m, b) for b in range(sink)]
            else:
                spots = [(sink + a, a, m - OPS_SRC + sink) for a in range(OPS_SRC)]
            for f, a, row in spots:
                first_sum, second_sum, third_sum = (
                    jnp.sum((value * phi_ref[f, k * ev : (k + 1) * ev]).reshape(ev // 8, 8, ev), axis=0)
                    for k, value in enumerate((both, zr, zi))
                )
                acc[a, 2 * row] = first_sum - third_sum
                acc[a, 2 * row + 1] = first_sum + second_sum
    lanes = lax.broadcasted_iota(jnp.int32, (4 * sink, ev), 1)
    total = jnp.zeros((4 * sink, ev), jnp.float32)
    for a in range(OPS_SRC):
        sums = jnp.sum(jnp.sum(acc[a], axis=1), axis=1, keepdims=True)
        total = jnp.where(lanes == a, sums, total)
    for b in range(sink):
        own_ref[b] = total[2 * b : 2 * b + 2, :OPS_SRC]
        other_ref[b] = total[2 * (sink + b) : 2 * (sink + b) + 2, :OPS_SRC]


def shards(perambulators, elementals, elem_place, op_lists):
    size = lax.axis_size("tm")
    half = size // 2
    me = lax.axis_index("tm")
    upper = (me >= half).astype(jnp.int32)
    across = [(source, (source + half) % size) for source in range(size)]

    def flip(value, bit):
        return lax.ppermute(value, "tm", [(source, source ^ bit) for source in range(size)])

    def spread(first):
        pieces, bit = [first], half // 2
        while bit:
            pieces += [flip(piece, bit) for piece in pieces]
            if len(pieces) > 8:
                pieces = [jnp.concatenate(pieces[at : at + 2]) for at in range(0, len(pieces), 2)]
            bit //= 2
        return pieces

    list_len = op_lists.shape[1]
    sink = list_len - OPS_SRC
    per_owner, _, ev, _ = elementals.shape
    order = perambulators.shape[2]
    spins = order // ev

    base = per_owner * 2 * ev
    pairs = op_lists.shape[0]
    wide = ((0, 8 - pairs), (0, ev - list_len))
    high = jnp.pad(lax.shift_right_logical(op_lists, 8).astype(jnp.bfloat16), wide)
    low = jnp.pad(lax.bitwise_and(op_lists, 255).astype(jnp.bfloat16), wide)
    block = jnp.concatenate([elementals.reshape(base, ev), high, low])[None]
    far_block = lax.ppermute(block, "tm", across)
    pieces = spread(block) + spread(far_block)
    far_digits = far_block[0, base:].astype(jnp.int32)
    other_list = far_digits[:pairs, :list_len] * 256 + far_digits[8 : 8 + pairs, :list_len]
    kept = lax.dynamic_index_in_dim(perambulators, upper, 0, keepdims=False)
    tau_t = kept.reshape(2, spins, ev, order).transpose(1, 3, 0, 2).reshape(spins, order, 2 * ev)
    tau_t, held = lax.optimization_barrier((tau_t, perambulators))
    rows = held.reshape(-1, 2, spins, ev, order)
    split = spins - 1

    def sent(first, count):
        return lax.dynamic_slice(rows, (1 - upper, 0, first, 0, 0), (1, 2, count, ev, order))[0]

    mu_a = lax.ppermute(sent(0, split), "tm", across)
    mu_b = lax.ppermute(sent(split, spins - split), "tm", across)

    ops = jnp.concatenate(
        [
            lax.dynamic_index_in_dim(op_lists, upper, 0, keepdims=False),
            lax.dynamic_index_in_dim(other_list, upper, 0, keepdims=False),
        ]
    )
    entries = (
        list(range(OPS_SRC))
        + list(range(list_len + OPS_SRC, 2 * list_len))
        + list(range(OPS_SRC, list_len))
        + list(range(list_len, list_len + OPS_SRC))
    )
    smem = pl.BlockSpec(memory_space=pltpu.SMEM)
    vmem = pl.BlockSpec(memory_space=pltpu.VMEM)
    anyspace = pl.BlockSpec(memory_space=pl.ANY)
    width = list_len * ev
    depth = 2 * order
    w, phi = pl.pallas_call(
        functools.partial(apply_kernel, per_owner=per_owner, half=half),
        out_shape=(
            jax.ShapeDtypeStruct((spins, width, depth), jnp.bfloat16),
            jax.ShapeDtypeStruct((list_len, 3 * ev, ev), jnp.float32),
        ),
        in_specs=[smem] * 4 + [vmem] + [anyspace] * len(pieces),
        out_specs=(vmem, vmem),
        scratch_shapes=[
            pltpu.VMEM((2 * list_len, 2 * ev, ev), jnp.bfloat16),
            pltpu.SemaphoreType.DMA((2 * list_len,)),
        ],
        compiler_params=pltpu.CompilerParams(vmem_limit_bytes=24 << 20),
        cost_estimate=pl.CostEstimate(
            flops=2 * spins * width * depth * 2 * ev, bytes_accessed=2 * spins * width * depth, transcendentals=0
        ),
        name="apply",
    )(jnp.array(entries, jnp.int32), ops, elem_place, me[None], tau_t, *pieces)
    z = pl.pallas_call(
        functools.partial(early_kernel, ev=ev),
        out_shape=jax.ShapeDtypeStruct((width, 2 * ev), jnp.float32),
        in_specs=[vmem] * 2,
        out_specs=vmem,
        compiler_params=pltpu.CompilerParams(vmem_limit_bytes=20 << 20),
        cost_estimate=pl.CostEstimate(
            flops=2 * spins * width * depth * 2 * ev, bytes_accessed=2 * spins * width * depth, transcendentals=0
        ),
        name="early",
    )(w, mu_a)
    small = jax.ShapeDtypeStruct((sink, 2, OPS_SRC), jnp.float32)
    own, other = pl.pallas_call(
        functools.partial(last_kernel, entries=list_len, first_spin=split),
        out_shape=(small, small),
        in_specs=[vmem] * 4,
        out_specs=(vmem, vmem),
        scratch_shapes=[pltpu.VMEM((OPS_SRC, 4 * sink, 8, ev), jnp.float32)],
        compiler_params=pltpu.CompilerParams(vmem_limit_bytes=20 << 20),
        cost_estimate=pl.CostEstimate(flops=2 * width * depth * ev, bytes_accessed=8 * width * ev, transcendentals=0),
        name="last",
    )(w, mu_b, z, phi)
    back = lax.ppermute(other, "tm", across)
    both = jnp.where(upper == 0, jnp.stack([own, back]), jnp.stack([back, own]))
    return both.transpose(0, 2, 3, 1)


def solution(mesh):
    return jax.shard_map(
        shards,
        mesh=mesh,
        in_specs=(
            P(("cfg", "tm"), None, None, None),
            P(("cfg", "tm"), None, None, None),
            P("cfg"),
            P(("cfg", "tm"), None),
        ),
        out_specs=P(("cfg", "tm"), None, None, None),
        check_vma=False,
    )
```

```python
import functools

import jax
import jax.numpy as jnp
from jax import lax
from jax.experimental import pallas as pl
from jax.experimental.pallas import tpu as pltpu
from jax.sharding import PartitionSpec as P

OPS_SRC = 6
NT = (((1,), (1,)), ((), ()))


def apply_kernel(src, ops, place, self_id, tau_t, *refs, per_owner, half):
    *pieces, w_ref, phi_ref, buf, sem = refs
    count = ops.shape[0]
    spins, order, twice = tau_t.shape
    ev = twice // 2
    steps = half.bit_length() - 1
    each = pieces[0].shape[0]

    def fetch(slot, _):
        row = place[ops[src[slot]]]
        owner = lax.div(row, per_owner)
        apart = lax.bitwise_xor(owner, self_id[0])
        index = half * (apart >= half).astype(jnp.int32)
        for step in range(steps):
            bit = lax.bitwise_and(lax.shift_right_logical(apart, jnp.int32(steps - 1 - step)), 1)
            index = index + bit * (1 << step)
        start = pl.multiple_of((row - owner * per_owner) * twice, twice)
        which = lax.div(index, each)

        def choose(low, high):
            if high - low == 1:
                source = pieces[low].at[index - low * each, pl.ds(start, twice)]
                pltpu.make_async_copy(source, buf.at[slot], sem.at[slot]).start()
                return
            middle = (low + high) // 2
            pl.when(which < middle)(functools.partial(choose, low, middle))
            pl.when(which >= middle)(functools.partial(choose, middle, high))

        choose(0, len(pieces))
        return 0

    def arrive(slot):
        pltpu.make_async_copy(pieces[0].at[0, pl.ds(0, twice)], buf.at[slot], sem.at[slot]).wait()

    lax.fori_loop(0, count, fetch, 0)
    for m in range(count // 2):
        arrive(m)
    for m in range(count // 2):
        real, imag = buf[m, :ev], buf[m, ev:]
        lifted = jnp.concatenate(
            [jnp.concatenate([real, -imag], axis=1), jnp.concatenate([imag, real], axis=1)], axis=0
        )
        for inner in range(spins):
            out = lax.dot_general(tau_t[inner], lifted, NT, preferred_element_type=jnp.float32)
            out = out.astype(jnp.bfloat16)
            for outer in range(spins):
                w_ref[outer, m * ev : (m + 1) * ev, inner * twice : (inner + 1) * twice] = out[
                    outer * ev : (outer + 1) * ev
                ]
    for m in range(count // 2, count):
        arrive(m)
        real, imag = buf[m, :ev].astype(jnp.float32), buf[m, ev:].astype(jnp.float32)
        phi_ref[m - count // 2, :ev] = real
        phi_ref[m - count // 2, ev : 2 * ev] = imag - real
        phi_ref[m - count // 2, 2 * ev :] = real + imag


def lift_rows(mu, spins):
    ev = mu.shape[1]
    top, low = [], []
    for inner in range(spins):
        real = mu[0, :, inner * ev : (inner + 1) * ev]
        imag = mu[1, :, inner * ev : (inner + 1) * ev]
        top += [real, -imag]
        low += [imag, real]
    return jnp.concatenate([jnp.concatenate(top, axis=1), jnp.concatenate(low, axis=1)], axis=0)


def products(w_ref, mu_ref, first, rows):
    spins = w_ref.shape[0]
    total = None
    for s in range(mu_ref.shape[1]):
        lifted = lift_rows(mu_ref[:, s], spins)
        part = lax.dot_general(w_ref[first + s, rows], lifted, NT, preferred_element_type=jnp.float32)
        total = part if total is None else total + part
    return total


def early_kernel(w_ref, mu_ref, z_ref, *, ev):
    height = z_ref.shape[0]
    for at in range(0, height, 4 * ev):
        rows = slice(at, min(at + 4 * ev, height))
        z_ref[rows] = products(w_ref, mu_ref, 0, rows)


def last_kernel(w_ref, mu_ref, z_ref, phi_ref, own_ref, other_ref, acc, *, entries, first_spin):
    ev = mu_ref.shape[2]
    sink = entries - OPS_SRC
    for first in range(0, entries, 4):
        block = range(first, min(first + 4, entries))
        rows = slice(first * ev, (block[-1] + 1) * ev)
        z = z_ref[rows] + products(w_ref, mu_ref, first_spin, rows)
        for m in block:
            at = (m - first) * ev
            zr, zi = z[at : at + ev, :ev], z[at : at + ev, ev:]
            both = zr + zi
            if m < OPS_SRC:
                spots = [(b, m, b) for b in range(sink)]
            else:
                spots = [(sink + a, a, m - OPS_SRC + sink) for a in range(OPS_SRC)]
            for f, a, row in spots:
                first_sum, second_sum, third_sum = (
                    jnp.sum((value * phi_ref[f, k * ev : (k + 1) * ev]).reshape(ev // 8, 8, ev), axis=0)
                    for k, value in enumerate((both, zr, zi))
                )
                acc[a, 2 * row] = first_sum - third_sum
                acc[a, 2 * row + 1] = first_sum + second_sum
    lanes = lax.broadcasted_iota(jnp.int32, (4 * sink, ev), 1)
    total = jnp.zeros((4 * sink, ev), jnp.float32)
    for a in range(OPS_SRC):
        sums = jnp.sum(jnp.sum(acc[a], axis=1), axis=1, keepdims=True)
        total = jnp.where(lanes == a, sums, total)
    for b in range(sink):
        own_ref[b] = total[2 * b : 2 * b + 2, :OPS_SRC]
        other_ref[b] = total[2 * (sink + b) : 2 * (sink + b) + 2, :OPS_SRC]


def shards(perambulators, elementals, elem_place, op_lists):
    size = lax.axis_size("tm")
    half = size // 2
    me = lax.axis_index("tm")
    upper = (me >= half).astype(jnp.int32)
    across = [(source, (source + half) % size) for source in range(size)]

    def flip(value, bit):
        return lax.ppermute(value, "tm", [(source, source ^ bit) for source in range(size)])

    def spread(first):
        pieces, bit = [first], half // 2
        while bit:
            pieces += [flip(piece, bit) for piece in pieces]
            if len(pieces) > 8:
                pieces = [jnp.concatenate(pieces[at : at + 2]) for at in range(0, len(pieces), 2)]
            bit //= 2
        return pieces

    list_len = op_lists.shape[1]
    sink = list_len - OPS_SRC
    per_owner, _, ev, _ = elementals.shape
    order = perambulators.shape[2]
    spins = order // ev

    base = per_owner * 2 * ev
    pairs = op_lists.shape[0]
    wide = jnp.pad(op_lists, ((base, 16 - pairs), (0, ev - list_len)))
    shifted = jnp.pad(op_lists, ((base + 8, 8 - pairs), (0, ev - list_len)))
    digits = lax.shift_right_logical(wide, 8) + lax.bitwise_and(shifted, 255)
    inside = lax.broadcasted_iota(jnp.int32, (base + 16, ev), 0) < base
    body = jnp.pad(elementals.reshape(base, ev), ((0, 16), (0, 0)))
    block = jnp.where(inside, body, digits.astype(jnp.bfloat16))[None]
    far_block = lax.ppermute(block, "tm", across)
    pieces = spread(block) + spread(far_block)
    far_digits = far_block[0, base:].astype(jnp.int32)
    other_list = far_digits[:pairs, :list_len] * 256 + far_digits[8 : 8 + pairs, :list_len]
    kept = lax.dynamic_index_in_dim(perambulators, upper, 0, keepdims=False)
    tau_t = kept.reshape(2, spins, ev, order).transpose(1, 3, 0, 2).reshape(spins, order, 2 * ev)
    tau_t, held = lax.optimization_barrier((tau_t, perambulators))
    rows = held.reshape(-1, 2, spins, ev, order)
    split = spins - 1

    def sent(first, count):
        return lax.dynamic_slice(rows, (1 - upper, 0, first, 0, 0), (1, 2, count, ev, order))[0]

    mu_a = lax.ppermute(sent(0, split), "tm", across)
    mu_b = lax.ppermute(sent(split, spins - split), "tm", across)

    ops = jnp.concatenate(
        [
            lax.dynamic_index_in_dim(op_lists, upper, 0, keepdims=False),
            lax.dynamic_index_in_dim(other_list, upper, 0, keepdims=False),
        ]
    )
    entries = (
        list(range(OPS_SRC))
        + list(range(list_len + OPS_SRC, 2 * list_len))
        + list(range(OPS_SRC, list_len))
        + list(range(list_len, list_len + OPS_SRC))
    )
    smem = pl.BlockSpec(memory_space=pltpu.SMEM)
    vmem = pl.BlockSpec(memory_space=pltpu.VMEM)
    anyspace = pl.BlockSpec(memory_space=pl.ANY)
    width = list_len * ev
    depth = 2 * order
    w, phi = pl.pallas_call(
        functools.partial(apply_kernel, per_owner=per_owner, half=half),
        out_shape=(
            jax.ShapeDtypeStruct((spins, width, depth), jnp.bfloat16),
            jax.ShapeDtypeStruct((list_len, 3 * ev, ev), jnp.float32),
        ),
        in_specs=[smem] * 4 + [vmem] + [anyspace] * len(pieces),
        out_specs=(vmem, vmem),
        scratch_shapes=[
            pltpu.VMEM((2 * list_len, 2 * ev, ev), jnp.bfloat16),
            pltpu.SemaphoreType.DMA((2 * list_len,)),
        ],
        compiler_params=pltpu.CompilerParams(vmem_limit_bytes=24 << 20),
        cost_estimate=pl.CostEstimate(
            flops=2 * spins * width * depth * 2 * ev, bytes_accessed=2 * spins * width * depth, transcendentals=0
        ),
        name="apply",
    )(jnp.array(entries, jnp.int32), ops, elem_place, me[None], tau_t, *pieces)
    z = pl.pallas_call(
        functools.partial(early_kernel, ev=ev),
        out_shape=jax.ShapeDtypeStruct((width, 2 * ev), jnp.float32),
        in_specs=[vmem] * 2,
        out_specs=vmem,
        compiler_params=pltpu.CompilerParams(vmem_limit_bytes=20 << 20),
        cost_estimate=pl.CostEstimate(
            flops=2 * spins * width * depth * 2 * ev, bytes_accessed=2 * spins * width * depth, transcendentals=0
        ),
        name="early",
    )(w, mu_a)
    small = jax.ShapeDtypeStruct((sink, 2, OPS_SRC), jnp.float32)
    own, other = pl.pallas_call(
        functools.partial(last_kernel, entries=list_len, first_spin=split),
        out_shape=(small, small),
        in_specs=[vmem] * 4,
        out_specs=(vmem, vmem),
        scratch_shapes=[pltpu.VMEM((OPS_SRC, 4 * sink, 8, ev), jnp.float32)],
        compiler_params=pltpu.CompilerParams(vmem_limit_bytes=20 << 20),
        cost_estimate=pl.CostEstimate(flops=2 * width * depth * ev, bytes_accessed=8 * width * ev, transcendentals=0),
        name="last",
    )(w, mu_b, z, phi)
    back = lax.ppermute(other, "tm", across)
    both = jnp.where(upper == 0, jnp.stack([own, back]), jnp.stack([back, own]))
    return both.transpose(0, 2, 3, 1)


def solution(mesh):
    return jax.shard_map(
        shards,
        mesh=mesh,
        in_specs=(
            P(("cfg", "tm"), None, None, None),
            P(("cfg", "tm"), None, None, None),
            P("cfg"),
            P(("cfg", "tm"), None),
        ),
        out_specs=P(("cfg", "tm"), None, None, None),
        check_vma=False,
    )
```

```python
import functools

import jax
import jax.numpy as jnp
from jax import lax
from jax.experimental import pallas as pl
from jax.experimental.pallas import tpu as pltpu
from jax.sharding import PartitionSpec as P

OPS_SRC = 6
NT = (((1,), (1,)), ((), ()))


def apply_kernel(src, ops, place, self_id, tau_t, *refs, per_owner, half):
    *pieces, w_ref, late_ref, phi_ref, buf, sem = refs
    count = ops.shape[0]
    spins, order, twice = tau_t.shape
    ev = twice // 2
    steps = half.bit_length() - 1
    each = pieces[0].shape[0]

    def fetch(slot, _):
        row = place[ops[src[slot]]]
        owner = lax.div(row, per_owner)
        apart = lax.bitwise_xor(owner, self_id[0])
        index = half * (apart >= half).astype(jnp.int32)
        for step in range(steps):
            bit = lax.bitwise_and(lax.shift_right_logical(apart, jnp.int32(steps - 1 - step)), 1)
            index = index + bit * (1 << step)
        start = pl.multiple_of((row - owner * per_owner) * twice, twice)
        which = lax.div(index, each)

        def choose(low, high):
            if high - low == 1:
                source = pieces[low].at[index - low * each, pl.ds(start, twice)]
                pltpu.make_async_copy(source, buf.at[slot], sem.at[slot]).start()
                return
            middle = (low + high) // 2
            pl.when(which < middle)(functools.partial(choose, low, middle))
            pl.when(which >= middle)(functools.partial(choose, middle, high))

        choose(0, len(pieces))
        return 0

    def arrive(slot):
        pltpu.make_async_copy(pieces[0].at[0, pl.ds(0, twice)], buf.at[slot], sem.at[slot]).wait()

    lax.fori_loop(0, count, fetch, 0)
    for m in range(count // 2):
        arrive(m)
    for m in range(count // 2):
        real, imag = buf[m, :ev], buf[m, ev:]
        lifted = jnp.concatenate(
            [jnp.concatenate([real, -imag], axis=1), jnp.concatenate([imag, real], axis=1)], axis=0
        )
        for inner in range(spins):
            out = lax.dot_general(tau_t[inner], lifted, NT, preferred_element_type=jnp.float32)
            out = out.astype(jnp.bfloat16)
            for outer in range(spins):
                target = w_ref.at[outer] if outer < w_ref.shape[0] else late_ref.at[outer - w_ref.shape[0]]
                target[m * ev : (m + 1) * ev, inner * twice : (inner + 1) * twice] = out[
                    outer * ev : (outer + 1) * ev
                ]
    for m in range(count // 2, count):
        arrive(m)
        real, imag = buf[m, :ev].astype(jnp.float32), buf[m, ev:].astype(jnp.float32)
        phi_ref[m - count // 2, :ev] = real
        phi_ref[m - count // 2, ev : 2 * ev] = imag - real
        phi_ref[m - count // 2, 2 * ev :] = real + imag


def lift_rows(mu, spins):
    ev = mu.shape[1]
    top, low = [], []
    for inner in range(spins):
        real = mu[0, :, inner * ev : (inner + 1) * ev]
        imag = mu[1, :, inner * ev : (inner + 1) * ev]
        top += [real, -imag]
        low += [imag, real]
    return jnp.concatenate([jnp.concatenate(top, axis=1), jnp.concatenate(low, axis=1)], axis=0)


def products(w_ref, mu_ref, rows):
    spins = mu_ref.shape[3] // mu_ref.shape[2]
    total = None
    for s in range(mu_ref.shape[1]):
        lifted = lift_rows(mu_ref[:, s], spins)
        part = lax.dot_general(w_ref[s, rows], lifted, NT, preferred_element_type=jnp.float32)
        total = part if total is None else total + part
    return total


def early_kernel(w_ref, mu_ref, z_ref, *, ev):
    height = z_ref.shape[0]
    for at in range(0, height, 4 * ev):
        rows = slice(at, min(at + 4 * ev, height))
        z_ref[rows] = products(w_ref, mu_ref, rows)


def last_kernel(w_ref, mu_ref, z_ref, phi_ref, out_ref, acc, *, entries, mirrored):
    ev = mu_ref.shape[2]
    sink = entries - OPS_SRC
    begin, end = (OPS_SRC, entries) if mirrored else (0, OPS_SRC)
    for first in range(begin, end, 3):
        last = min(first + 3, end)
        rows = slice(first * ev, last * ev)
        z = z_ref[rows] + products(w_ref, mu_ref, rows)
        for m in range(first, last):
            at = (m - first) * ev
            zr, zi = z[at : at + ev, :ev], z[at : at + ev, ev:]
            both = zr + zi
            if mirrored:
                spots = [(sink + a, a, m - OPS_SRC) for a in range(OPS_SRC)]
            else:
                spots = [(b, m, b) for b in range(sink)]
            for f, a, row in spots:
                first_sum, second_sum, third_sum = (
                    jnp.sum((value * phi_ref[f, k * ev : (k + 1) * ev]).reshape(ev // 8, 8, ev), axis=0)
                    for k, value in enumerate((both, zr, zi))
                )
                acc[a, 2 * row] = first_sum - third_sum
                acc[a, 2 * row + 1] = first_sum + second_sum
    lanes = lax.broadcasted_iota(jnp.int32, (2 * sink, ev), 1)
    total = jnp.zeros((2 * sink, ev), jnp.float32)
    for a in range(OPS_SRC):
        sums = jnp.sum(jnp.sum(acc[a], axis=1), axis=1, keepdims=True)
        total = jnp.where(lanes == a, sums, total)
    for b in range(sink):
        out_ref[b] = total[2 * b : 2 * b + 2, :OPS_SRC]


def shards(perambulators, elementals, elem_place, op_lists):
    size = lax.axis_size("tm")
    half = size // 2
    me = lax.axis_index("tm")
    upper = (me >= half).astype(jnp.int32)
    across = [(source, (source + half) % size) for source in range(size)]

    def flip(value, bit):
        return lax.ppermute(value, "tm", [(source, source ^ bit) for source in range(size)])

    def spread(first):
        pieces, bit = [first], half // 2
        while bit:
            pieces += [flip(piece, bit) for piece in pieces]
            if len(pieces) > 8:
                pieces = [jnp.concatenate(pieces[at : at + 2]) for at in range(0, len(pieces), 2)]
            bit //= 2
        return pieces

    list_len = op_lists.shape[1]
    sink = list_len - OPS_SRC
    per_owner, _, ev, _ = elementals.shape
    order = perambulators.shape[2]
    spins = order // ev

    base = per_owner * 2 * ev
    pairs = op_lists.shape[0]
    wide = jnp.pad(op_lists, ((base, 16 - pairs), (0, ev - list_len)))
    shifted = jnp.pad(op_lists, ((base + 8, 8 - pairs), (0, ev - list_len)))
    digits = lax.shift_right_logical(wide, 8) + lax.bitwise_and(shifted, 255)
    inside = lax.broadcasted_iota(jnp.int32, (base + 16, ev), 0) < base
    body = jnp.pad(elementals.reshape(base, ev), ((0, 16), (0, 0)))
    block = jnp.where(inside, body, digits.astype(jnp.bfloat16))[None]
    far_block = lax.ppermute(block, "tm", across)
    pieces = spread(block) + spread(far_block)
    far_digits = far_block[0, base:].astype(jnp.int32)
    other_list = far_digits[:pairs, :list_len] * 256 + far_digits[8 : 8 + pairs, :list_len]
    kept = lax.dynamic_index_in_dim(perambulators, upper, 0, keepdims=False)
    tau_t = kept.reshape(2, spins, ev, order).transpose(1, 3, 0, 2).reshape(spins, order, 2 * ev)
    tau_t, held = lax.optimization_barrier((tau_t, perambulators))
    rows = held.reshape(-1, 2, spins, ev, order)
    split = spins - 1

    def sent(first, count):
        return lax.dynamic_slice(rows, (1 - upper, 0, first, 0, 0), (1, 2, count, ev, order))[0]

    mu_a = lax.ppermute(sent(0, split), "tm", across)
    mu_b = lax.ppermute(sent(split, spins - split), "tm", across)

    ops = jnp.concatenate(
        [
            lax.dynamic_index_in_dim(op_lists, upper, 0, keepdims=False),
            lax.dynamic_index_in_dim(other_list, upper, 0, keepdims=False),
        ]
    )
    entries = (
        list(range(OPS_SRC))
        + list(range(list_len + OPS_SRC, 2 * list_len))
        + list(range(OPS_SRC, list_len))
        + list(range(list_len, list_len + OPS_SRC))
    )
    smem = pl.BlockSpec(memory_space=pltpu.SMEM)
    vmem = pl.BlockSpec(memory_space=pltpu.VMEM)
    anyspace = pl.BlockSpec(memory_space=pl.ANY)
    width = list_len * ev
    depth = 2 * order
    w, w_late, phi = pl.pallas_call(
        functools.partial(apply_kernel, per_owner=per_owner, half=half),
        out_shape=(
            jax.ShapeDtypeStruct((split, width, depth), jnp.bfloat16),
            jax.ShapeDtypeStruct((spins - split, width, depth), jnp.bfloat16),
            jax.ShapeDtypeStruct((list_len, 3 * ev, ev), jnp.float32),
        ),
        in_specs=[smem] * 4 + [vmem] + [anyspace] * len(pieces),
        out_specs=(vmem, vmem, vmem),
        scratch_shapes=[
            pltpu.VMEM((2 * list_len, 2 * ev, ev), jnp.bfloat16),
            pltpu.SemaphoreType.DMA((2 * list_len,)),
        ],
        compiler_params=pltpu.CompilerParams(vmem_limit_bytes=24 << 20),
        cost_estimate=pl.CostEstimate(
            flops=2 * spins * width * depth * 2 * ev, bytes_accessed=2 * spins * width * depth, transcendentals=0
        ),
        name="apply",
    )(jnp.array(entries, jnp.int32), ops, elem_place, me[None], tau_t, *pieces)
    z = pl.pallas_call(
        functools.partial(early_kernel, ev=ev),
        out_shape=jax.ShapeDtypeStruct((width, 2 * ev), jnp.float32),
        in_specs=[vmem] * 2,
        out_specs=vmem,
        compiler_params=pltpu.CompilerParams(vmem_limit_bytes=20 << 20),
        cost_estimate=pl.CostEstimate(
            flops=2 * spins * width * depth * 2 * ev, bytes_accessed=2 * spins * width * depth, transcendentals=0
        ),
        name="early",
    )(w, mu_a)

    needed = [
        pl.BlockSpec((spins - split, OPS_SRC * ev, depth), lambda g: (0, 0, 0)),
        pl.BlockSpec((2, spins - split, ev, order), lambda g: (0, 0, 0, 0)),
        pl.BlockSpec((OPS_SRC * ev, 2 * ev), lambda g: (0, 0)),
        pl.BlockSpec((sink, 3 * ev, ev), lambda g: (0, 0, 0)),
    ]

    def correlate(mirrored):
        return pl.pallas_call(
            functools.partial(last_kernel, entries=list_len, mirrored=mirrored),
            out_shape=jax.ShapeDtypeStruct((sink, 2, OPS_SRC), jnp.float32),
            grid=(1,),
            in_specs=[vmem] * 4 if mirrored else needed,
            out_specs=vmem,
            scratch_shapes=[pltpu.VMEM((OPS_SRC, 2 * sink, 8, ev), jnp.float32)],
            compiler_params=pltpu.CompilerParams(vmem_limit_bytes=(20 if mirrored else 52) << 20),
            name="mirrored" if mirrored else "own",
        )(w_late, mu_b, z, phi)

    back = lax.ppermute(correlate(True), "tm", across)
    own = correlate(False)
    both = jnp.where(upper == 0, jnp.stack([own, back]), jnp.stack([back, own]))
    return both.transpose(0, 2, 3, 1)


def solution(mesh):
    return jax.shard_map(
        shards,
        mesh=mesh,
        in_specs=(
            P(("cfg", "tm"), None, None, None),
            P(("cfg", "tm"), None, None, None),
            P("cfg"),
            P(("cfg", "tm"), None),
        ),
        out_specs=P(("cfg", "tm"), None, None, None),
        check_vma=False,
    )
```
